32 devices in a mesh: grp: 2 (over x), bits: 16 (over z, y, core).
Axes of the slice: x: 2, y: 2, z: 4, core: 2. Of those that a mesh axis runs over, the one named last changes fastest.
Arguments:
- prefix: bfloat16 [128, 16, 1024], P(('grp', 'bits')), parts along dimension 0, may hold values from -6 to 6
- first_suffix: bfloat16 [8, 2, 512, 512], P('grp', None, 'bits'), parts along dimension 0, may hold values from -0.109375 to 0.109375
- pair_prefix: int32 [256, 3], P(('grp', 'bits')), parts along dimension 0, may hold values from 0 to 3
- pair_suffix: int32 [256, 3], P(('grp', 'bits')), parts along dimension 0, may hold values from 0 to 3, all different within a row
- merge_count: int32 [256], P(('grp', 'bits')), parts along dimension 0, may hold values from 1 to 3, as said below
- suffix: bfloat16 [32, 2, 512, 512], P(('grp', 'bits')), parts along dimension 0, may hold values from -0.1875 to 0.1875
- routes: int32 [256, 12], P(('grp', 'bits')), parts along dimension 0, may hold values from 0 to 15, all different within a row; in each aligned block of 8 rows (0 to 7, 8 to 15, ...) at most 8 rows name the same one
- cap: bfloat16 [2, 512, 64], replicated, may hold values from -0.0546875 to 0.0546875
Outputs:
- capped: float32 [256, 16, 128], P(('grp', 'bits')), parts along dimension 0
The draws below stay inside these ranges and needn't reach their ends.
There are 2 independent parts, one for each index of `grp`. The reference program is written for one: setup_inputs(seed, part) draws one part's arguments, and reference() takes and returns one part's arrays. A program takes and returns all parts, laid end to end along the dimension named above; an argument that names none is the same for every part. Nothing has to cross between parts.
Inputs may be any that keep to these rules, and one draw needn't show every extreme that they name: `pair_suffix`: each row names 3 different lifetime-one blocks. `merge_count`: some piece has exactly 3 merges and some exactly one. `routes`: each row names 12 different suffixes; in each aligned block of 8 rows no suffix is named by more than 8 rows, a bound that some block reaches.
All inputs are finite; a program needn't handle non-finite values.
Results may differ from the reference program's by a relative error of at most 0.005.
Values may be sent and summed in bfloat16 or wider, within the bound.
A program may use at most 64 MiB of HBM per device.

```python
import math
import jax
import jax.numpy as jnp
import numpy as np
from jax import lax

W = 512
CAPW = 64
PR = 16
PIECES_DEV = 8
PRE_DEV = 4
NA = 4
K1 = 3
TOP = 12
NSUF = 16
PIECES = 128
NPRE = 64
MOST = 8


def draw_merge_count(key, part):
    counts = jax.random.randint(key, (PIECES,), 1, K1 + 1)
    chosen = jax.random.randint(jax.random.fold_in(key, 7), (), 0, PIECES)
    counts = counts.at[chosen].set(K1)
    counts = counts.at[(chosen + 1) % PIECES].set(1)
    return counts.astype(jnp.int32)


def touch_ends(array, own_key, low, high):
    longest = array.shape.index(max(array.shape))
    spots = []
    for shift in (0, 1):
        where = [jax.random.randint(jax.random.fold_in(own_key, axis), (), 0, length) for axis, length in enumerate(array.shape)]
        where[longest] = (where[longest] + shift) % array.shape[longest]
        spots.append(tuple(where))
    return array.at[spots[0]].set(low).at[spots[1]].set(high)


def level_of(key, shape, cuts, least, high):
    gain = 1.0
    for axis_at, blocks in cuts:
        heights = jax.random.uniform(jax.random.fold_in(jax.random.fold_in(key, 6), axis_at), (blocks,), jnp.float32, least / len(cuts), high / len(cuts))
        gain = gain * jnp.repeat(jnp.exp(heights), shape[axis_at] // blocks).reshape((-1,) + (1,) * (len(shape) - 1 - axis_at))
    return gain


def picks_of(own_key, rows, amount, top, lift):
    order = jax.random.permutation(jax.random.fold_in(own_key, 1), amount)
    favour = order
    for power in range(3):
        favour = favour * favour // amount
    favour = favour * lift // amount
    chance = jax.random.randint(jax.random.fold_in(own_key, 2), (rows, amount), 0, 4096) + favour
    fixed_rows = jax.random.permutation(jax.random.fold_in(own_key, 3), rows)[jnp.arange(amount) % rows]
    chance = jnp.where(jnp.arange(rows)[:, None] == fixed_rows[None, :], 1 << 14, chance)
    score = chance * amount + jnp.arange(amount)
    return lax.top_k(score.astype(jnp.int32), top)[1].astype(jnp.int32)


def routed_block(key, own, number, rows, number_of, top, bound, slope):
    order = jax.random.permutation(key, number_of)
    crowded, ordinary = portions_of(number_of, rows * top, bound, slope, True), portions_of(number_of, rows * top, bound, slope, False)
    places = jnp.arange(number_of)

    def named(sizes, turn):
        used = int((sizes > 0).sum())
        fixed = max(1, used // 4)
        passed = fixed + (places - fixed + turn * (used - fixed)) % max(1, number_of - fixed)
        return jnp.zeros((number_of,), jnp.int32).at[order[jnp.where(places < fixed, places, passed)]].set(jnp.asarray(sizes, jnp.int32))

    sizes = jnp.where(number % 4 == 0, named(crowded, number // 4), named(ordinary, number - number // 4 - 1))
    mixed = jax.random.permutation(jax.random.fold_in(own, 3), number_of)
    donor, taker = mixed[0:number_of // 2 * 2:2], mixed[1:number_of // 2 * 2:2]
    margin = jnp.minimum(sizes[donor] - 1, bound - sizes[taker]) // 2
    margin = jnp.where((donor == order[0]) | (taker == order[0]) | (sizes[taker] == 0), 0, jnp.maximum(margin, 0))
    passed = jax.random.randint(jax.random.fold_in(own, 4), (number_of // 2,), 0, 1 << 20) % (margin + 1)
    sizes = sizes.at[donor].add(-passed).at[taker].add(passed)
    items = jnp.searchsorted(jnp.cumsum(sizes), jnp.arange(rows * top), side="right").astype(jnp.int32)
    listing = items.reshape(top, rows).T
    listing = listing[jax.random.permutation(jax.random.fold_in(own, 1), rows)]
    turn = jax.random.randint(jax.random.fold_in(own, 2), (rows, 1), 0, top)
    return jnp.take_along_axis(listing, (jnp.arange(top)[None, :] + turn) % top, axis=1)


def portions_of(amount, total, reach, lean, full):
    portions = [(1 << 20) // math.isqrt(rank ** lean) + 1 for rank in range(1, amount + 1)]
    largest = reach if full else min(reach, max(-(-total // amount), total * portions[0] // sum(portions)))
    least = 1 if total - largest >= amount - 1 else 0
    given, surplus = [largest] + [least] * (amount - 1), total - largest - least * (amount - 1)
    while surplus > 0:
        free = [i for i in range(1, amount) if given[i] < largest] or [i for i in range(1, amount) if given[i] < reach]
        pool, left = sum([portions[i] for i in free]), surplus
        for i in free:
            extra = min(reach - given[i], max(1, left * portions[i] // pool), surplus)
            given[i] = given[i] + extra
            surplus = surplus - extra
    return np.array(given)


def centred(stream_key, extent, spread, bound, shards=(), held_as=jnp.bfloat16):
    entries = jax.random.normal(stream_key, extent, jnp.float32) * spread
    if len(shards) > 0:
        entries = level_of(stream_key, extent, shards, -0.22, 0.18) * entries
    return jnp.clip(entries, min=-bound, max=bound).astype(held_as)


def setup_inputs(seed: int = 0, part: int = 0) -> dict:
    arg_keys = jax.random.split(jax.random.key(seed), 9)
    part_keys = jax.random.split(jax.random.fold_in(arg_keys[8], part), 9)
    prefix = centred(part_keys[0], (NPRE, PR, 2 * W), 1.0, 6.0, ((0, 16),))
    first_suffix = centred(part_keys[1], (NA, 2, W, W), (2 * W * K1) ** -0.5, 0.109375, ((2, 16),))
    pair_prefix = touch_ends(jax.random.randint(part_keys[2], (PIECES, K1), 0, PRE_DEV), jax.random.fold_in(part_keys[2], 1), 0, PRE_DEV - 1).astype(jnp.int32)
    pair_suffix = picks_of(part_keys[3], PIECES, NA, K1, 0)
    merge_count = draw_merge_count(jax.random.fold_in(jax.random.fold_in(arg_keys[8], part), 71), part)
    suffix = centred(part_keys[5], (NSUF, 2, W, W), (2 * W) ** -0.5, 0.1875, ((0, 16),))
    routes_keys = jax.random.split(jax.random.fold_in(part_keys[6], 1), PIECES // PIECES_DEV)
    routes_turns = jax.random.permutation(jax.random.fold_in(part_keys[6], 3), PIECES // PIECES_DEV)
    routes = jax.vmap(lambda own, number: routed_block(jax.random.fold_in(part_keys[6], 2), own, number, PIECES_DEV, NSUF, TOP, MOST, 2))(routes_keys, routes_turns).reshape((PIECES, TOP))
    cap = centred(arg_keys[7], (2, W, CAPW), (2 * W * TOP) ** -0.5, 0.0546875)
    return dict(prefix=prefix, first_suffix=first_suffix, pair_prefix=pair_prefix, pair_suffix=pair_suffix, merge_count=merge_count, suffix=suffix, routes=routes, cap=cap)


HIGHEST_PRECISION = lax.Precision.HIGHEST


def complex_form(blocks):
    real_part = blocks[..., 0, :, :]
    imag_part = blocks[..., 1, :, :]
    upper_half = jnp.concatenate([real_part, imag_part], axis=-1)
    lower_half = jnp.concatenate([-imag_part, real_part], axis=-1)
    return jnp.concatenate([upper_half, lower_half], axis=-2)


def reference(prefix, first_suffix, pair_prefix, pair_suffix, merge_count, suffix, routes, cap):
    first_forms = complex_form(first_suffix.astype(jnp.float32))
    cap_form = complex_form(cap.astype(jnp.float32))

    def one_piece(piece_index):
        owner_index = piece_index // PIECES_DEV
        prefix_rows = prefix[PRE_DEV * owner_index + pair_prefix[piece_index]].astype(jnp.float32)
        block_forms = first_forms[pair_suffix[piece_index]]
        live_mask = (jnp.arange(K1, dtype=jnp.int32) < merge_count[piece_index]).astype(jnp.float32)
        merge_terms = jnp.einsum("krc,kcw->krw", prefix_rows, block_forms, precision=HIGHEST_PRECISION)
        state_rows = jnp.sum(merge_terms * live_mask[:, None, None], axis=0).astype(jnp.bfloat16)
        state_rows = lax.optimization_barrier(state_rows).astype(jnp.float32)
        chosen = complex_form(suffix[routes[piece_index]].astype(jnp.float32))
        partial_value = jnp.einsum("rc,kcw->krw", state_rows, chosen, precision=HIGHEST_PRECISION).astype(jnp.bfloat16)
        partial_value = lax.optimization_barrier(partial_value).astype(jnp.float32)
        merged = jnp.sum(partial_value, axis=0)
        return jnp.dot(merged, cap_form, precision=HIGHEST_PRECISION)

    return lax.map(one_piece, jnp.arange(PIECES, dtype=jnp.int32))
```

```python
import jax
import jax.numpy as jnp
from jax import lax
from jax.sharding import PartitionSpec as P

HIGHEST_PRECISION = lax.Precision.HIGHEST


def complex_form(blocks):
    real_part = blocks[..., 0, :, :]
    imag_part = blocks[..., 1, :, :]
    upper_half = jnp.concatenate([real_part, imag_part], axis=-1)
    lower_half = jnp.concatenate([-imag_part, real_part], axis=-1)
    return jnp.concatenate([upper_half, lower_half], axis=-2)


def on_device_sparse(prefix, first_suffix, pair_prefix, pair_suffix, merge_count, suffix, routes, cap):
    pieces = pair_prefix.shape[0]
    merges = pair_prefix.shape[1]
    held_blocks = prefix.shape[0]
    rows_piece = prefix.shape[1]
    twice_width = prefix.shape[2]
    half_width = twice_width // 2
    first_count = first_suffix.shape[0]
    listed = routes.shape[1]
    owners = lax.axis_size("bits")
    slot_count = min(pieces, max(2, (2 * pieces * listed + owners - 1) // owners))
    live_mask = lax.broadcasted_iota(jnp.int32, (pieces, merges), 1) < merge_count[:, None]
    matches = (
        pair_suffix[:, :, None] == lax.broadcasted_iota(jnp.int32, (pieces, merges, first_count), 2)
    ) & live_mask[:, :, None]
    which_block = pair_prefix[:, :, None] == lax.broadcasted_iota(
        jnp.int32, (pieces, merges, held_blocks), 2
    )
    prefix_picks = jnp.einsum(
        "ika,ikp->iap", matches.astype(jnp.float32), which_block.astype(jnp.float32)
    ).astype(jnp.bfloat16)
    selected = jnp.einsum(
        "iap,prc->airc", prefix_picks, prefix, preferred_element_type=jnp.float32
    ).astype(jnp.bfloat16)
    selected = selected.reshape(first_count, pieces * rows_piece, twice_width)
    portion = lax.all_gather(first_suffix, "bits", axis=2, tiled=True)
    count_rows = portion.shape[2]
    real_cols = lax.slice_in_dim(selected, 0, count_rows, axis=2)
    imag_cols = lax.dynamic_slice_in_dim(selected, half_width, count_rows, 2)
    left_side = jnp.concatenate([real_cols, imag_cols], axis=2)
    upper_half = jnp.concatenate([portion[:, 0], portion[:, 1]], axis=2)
    lower_half = jnp.concatenate([-portion[:, 1], portion[:, 0]], axis=2)
    right_side = jnp.concatenate([upper_half, lower_half], axis=1)
    state_rows = jnp.einsum(
        "arc,acw->rw", left_side, right_side, preferred_element_type=jnp.float32
    )
    state_rows = state_rows.astype(jnp.bfloat16).reshape(pieces, rows_piece, twice_width)
    named_by = jnp.sum(
        (routes[:, :, None] == lax.broadcasted_iota(jnp.int32, (pieces, listed, owners), 2)).astype(
            jnp.int32
        ),
        axis=1,
    )
    slot_rank = jnp.cumsum(named_by, axis=0) - named_by
    slot_hit = (
        slot_rank[:, :, None] == lax.broadcasted_iota(jnp.int32, (pieces, owners, slot_count), 2)
    ) & (named_by[:, :, None] > 0)
    dispatch = jnp.transpose(slot_hit, (1, 2, 0)).astype(jnp.bfloat16)
    outgoing = jnp.einsum(
        "dmi,irc->dmrc", dispatch, state_rows, preferred_element_type=jnp.float32
    ).astype(jnp.bfloat16)
    own_form = complex_form(suffix[0])
    cap_form = complex_form(cap)
    products = jnp.einsum(
        "smrc,cw->smrw",
        lax.all_to_all(outgoing, "bits", split_axis=0, concat_axis=0, tiled=True),
        own_form,
        preferred_element_type=jnp.float32,
    ).astype(jnp.bfloat16)
    capped_terms = jnp.einsum(
        "smrw,wv->smrv", products, cap_form, preferred_element_type=jnp.float32
    )
    returned = lax.all_to_all(
        capped_terms.astype(jnp.bfloat16), "bits", split_axis=0, concat_axis=0, tiled=True
    ).astype(capped_terms.dtype)
    return jnp.einsum(
        "dmi,dmrv->irv", dispatch.astype(jnp.float32), returned, precision=HIGHEST_PRECISION
    )


def weights_of(pair_prefix, pair_suffix, merge_count, held_blocks, first_count):
    pieces, merges = pair_prefix.shape
    live_mask = lax.broadcasted_iota(jnp.int32, (pieces, merges), 1) < merge_count[:, None]
    matches = (
        pair_suffix[:, :, None] == lax.broadcasted_iota(jnp.int32, (pieces, merges, first_count), 2)
    ) & live_mask[:, :, None]
    which_block = pair_prefix[:, :, None] == lax.broadcasted_iota(
        jnp.int32, (pieces, merges, held_blocks), 2
    )
    return jnp.sum(
        (matches[:, :, :, None] & which_block[:, :, None, :]).astype(jnp.float32), axis=1
    ).astype(jnp.bfloat16)


def on_device_dense(prefix, first_suffix, pair_prefix, pair_suffix, merge_count, suffix, routes, cap):
    pieces = pair_prefix.shape[0]
    held_blocks, rows_piece, twice_width = prefix.shape
    first_count = first_suffix.shape[0]
    owners = lax.axis_size("bits")
    listed = routes.shape[1]
    portion = lax.all_gather(first_suffix, "bits", axis=2, tiled=True)
    cap_form = jnp.concatenate([cap[0], cap[1]], axis=1)
    cap_turn = jnp.concatenate([-cap[1], cap[0]], axis=1)
    closed = (
        jnp.dot(suffix[0, 0], cap_form, preferred_element_type=jnp.float32)
        + jnp.dot(suffix[0, 1], cap_turn, preferred_element_type=jnp.float32)
    ).astype(jnp.bfloat16)
    closed_all = lax.all_gather(closed, "bits", axis=1, tiled=False)
    picks = weights_of(pair_prefix, pair_suffix, merge_count, held_blocks, first_count)
    selected = jnp.einsum(
        "iap,prc->airc", picks, prefix, preferred_element_type=jnp.float32
    ).astype(jnp.bfloat16)
    selected = selected.reshape(first_count, pieces * rows_piece, twice_width)
    half = twice_width // 2
    real = selected[:, :, :half]
    imag = selected[:, :, half:]
    by_real = jnp.einsum(
        "arc,acw->rw", jnp.concatenate([real, -imag], axis=2),
        portion.reshape(first_count, twice_width, half), preferred_element_type=jnp.float32,
    )
    by_imag = jnp.einsum(
        "arc,acw->rw", jnp.concatenate([imag, real], axis=2),
        portion.reshape(first_count, twice_width, half), preferred_element_type=jnp.float32,
    )
    state_real = by_real.astype(jnp.bfloat16)
    state_imag = by_imag.astype(jnp.bfloat16)
    flat = closed_all.reshape(half, -1)
    capw = cap.shape[2]
    stacked = jnp.concatenate([state_real, state_imag], axis=0)
    both = jnp.dot(stacked, flat, preferred_element_type=jnp.float32)
    both = both.reshape(2, pieces, rows_piece, owners, 2, capw)
    named = jnp.sum(
        (routes[:, :, None] == lax.broadcasted_iota(jnp.int32, (pieces, listed, owners), 2)).astype(
            jnp.float32
        ),
        axis=1,
    )
    summed = jnp.sum(both * named[None, :, None, :, None, None], axis=3)
    out_real = summed[0, :, :, 0] - summed[1, :, :, 1]
    out_imag = summed[0, :, :, 1] + summed[1, :, :, 0]
    return jnp.concatenate([out_real, out_imag], axis=-1)


def on_device(prefix, first_suffix, pair_prefix, pair_suffix, merge_count, suffix, routes, cap):
    pieces = pair_prefix.shape[0]
    listed = routes.shape[1]
    owners = lax.axis_size("bits")
    slots = min(pieces, max(2, (2 * pieces * listed + owners - 1) // owners))
    body = on_device_dense if slots == pieces else on_device_sparse
    return body(
        prefix, first_suffix, pair_prefix, pair_suffix, merge_count, suffix, routes, cap
    )


def solution(mesh):
    return jax.shard_map(
        on_device,
        mesh=mesh,
        in_specs=(
            P(("grp", "bits"), None, None),
            P("grp", None, "bits", None),
            P(("grp", "bits"), None),
            P(("grp", "bits"), None),
            P(("grp", "bits")),
            P(("grp", "bits"), None, None, None),
            P(("grp", "bits"), None),
            P(),
        ),
        out_specs=P(("grp", "bits"), None, None),
        check_vma=False,
    )
```

```python
import jax
import jax.numpy as jnp
from jax import lax
from jax.experimental import pallas as pl
from jax.experimental.pallas import tpu as pltpu
from jax.sharding import PartitionSpec as P

HIGHEST_PRECISION = lax.Precision.HIGHEST


def complex_form(blocks):
    real_part = blocks[..., 0, :, :]
    imag_part = blocks[..., 1, :, :]
    upper_half = jnp.concatenate([real_part, imag_part], axis=-1)
    lower_half = jnp.concatenate([-imag_part, real_part], axis=-1)
    return jnp.concatenate([upper_half, lower_half], axis=-2)


def on_device_sparse(prefix, first_suffix, pair_prefix, pair_suffix, merge_count, suffix, routes, cap):
    pieces = pair_prefix.shape[0]
    merges = pair_prefix.shape[1]
    held_blocks = prefix.shape[0]
    rows_piece = prefix.shape[1]
    twice_width = prefix.shape[2]
    half_width = twice_width // 2
    first_count = first_suffix.shape[0]
    listed = routes.shape[1]
    owners = lax.axis_size("bits")
    slot_count = min(pieces, max(2, (2 * pieces * listed + owners - 1) // owners))
    live_mask = lax.broadcasted_iota(jnp.int32, (pieces, merges), 1) < merge_count[:, None]
    matches = (
        pair_suffix[:, :, None] == lax.broadcasted_iota(jnp.int32, (pieces, merges, first_count), 2)
    ) & live_mask[:, :, None]
    which_block = pair_prefix[:, :, None] == lax.broadcasted_iota(
        jnp.int32, (pieces, merges, held_blocks), 2
    )
    prefix_picks = jnp.einsum(
        "ika,ikp->iap", matches.astype(jnp.float32), which_block.astype(jnp.float32)
    ).astype(jnp.bfloat16)
    selected = jnp.einsum(
        "iap,prc->airc", prefix_picks, prefix, preferred_element_type=jnp.float32
    ).astype(jnp.bfloat16)
    selected = selected.reshape(first_count, pieces * rows_piece, twice_width)
    portion = lax.all_gather(first_suffix, "bits", axis=2, tiled=True)
    count_rows = portion.shape[2]
    real_cols = lax.slice_in_dim(selected, 0, count_rows, axis=2)
    imag_cols = lax.dynamic_slice_in_dim(selected, half_width, count_rows, 2)
    left_side = jnp.concatenate([real_cols, imag_cols], axis=2)
    upper_half = jnp.concatenate([portion[:, 0], portion[:, 1]], axis=2)
    lower_half = jnp.concatenate([-portion[:, 1], portion[:, 0]], axis=2)
    right_side = jnp.concatenate([upper_half, lower_half], axis=1)
    state_rows = jnp.einsum(
        "arc,acw->rw", left_side, right_side, preferred_element_type=jnp.float32
    )
    state_rows = state_rows.astype(jnp.bfloat16).reshape(pieces, rows_piece, twice_width)
    named_by = jnp.sum(
        (routes[:, :, None] == lax.broadcasted_iota(jnp.int32, (pieces, listed, owners), 2)).astype(
            jnp.int32
        ),
        axis=1,
    )
    slot_rank = jnp.cumsum(named_by, axis=0) - named_by
    slot_hit = (
        slot_rank[:, :, None] == lax.broadcasted_iota(jnp.int32, (pieces, owners, slot_count), 2)
    ) & (named_by[:, :, None] > 0)
    dispatch = jnp.transpose(slot_hit, (1, 2, 0)).astype(jnp.bfloat16)
    outgoing = jnp.einsum(
        "dmi,irc->dmrc", dispatch, state_rows, preferred_element_type=jnp.float32
    ).astype(jnp.bfloat16)
    own_form = complex_form(suffix[0])
    cap_form = complex_form(cap)
    products = jnp.einsum(
        "smrc,cw->smrw",
        lax.all_to_all(outgoing, "bits", split_axis=0, concat_axis=0, tiled=True),
        own_form,
        preferred_element_type=jnp.float32,
    ).astype(jnp.bfloat16)
    capped_terms = jnp.einsum(
        "smrw,wv->smrv", products, cap_form, preferred_element_type=jnp.float32
    )
    returned = lax.all_to_all(
        capped_terms.astype(jnp.bfloat16), "bits", split_axis=0, concat_axis=0, tiled=True
    ).astype(capped_terms.dtype)
    return jnp.einsum(
        "dmi,dmrv->irv", dispatch.astype(jnp.float32), returned, precision=HIGHEST_PRECISION
    )


def weights_of(pair_prefix, pair_suffix, merge_count, held_blocks, first_count):
    pieces, merges = pair_prefix.shape
    live_mask = lax.broadcasted_iota(jnp.int32, (pieces, merges), 1) < merge_count[:, None]
    matches = (
        pair_suffix[:, :, None] == lax.broadcasted_iota(jnp.int32, (pieces, merges, first_count), 2)
    ) & live_mask[:, :, None]
    which_block = pair_prefix[:, :, None] == lax.broadcasted_iota(
        jnp.int32, (pieces, merges, held_blocks), 2
    )
    return jnp.sum(
        (matches[:, :, :, None] & which_block[:, :, None, :]).astype(jnp.float32), axis=1
    ).astype(jnp.bfloat16)


def on_device_dense(prefix, first_suffix, pair_prefix, pair_suffix, merge_count, suffix, routes, cap):
    pieces = pair_prefix.shape[0]
    held_blocks, rows_piece, twice_width = prefix.shape
    first_count = first_suffix.shape[0]
    owners = lax.axis_size("bits")
    listed = routes.shape[1]
    portion = lax.all_gather(first_suffix, "bits", axis=2, tiled=True)
    cap_form = jnp.concatenate([cap[0], cap[1]], axis=1)
    cap_turn = jnp.concatenate([-cap[1], cap[0]], axis=1)
    closed = (
        jnp.dot(suffix[0, 0], cap_form, preferred_element_type=jnp.float32)
        + jnp.dot(suffix[0, 1], cap_turn, preferred_element_type=jnp.float32)
    ).astype(jnp.bfloat16)
    closed_all = lax.all_gather(closed, "bits", axis=1, tiled=False)
    picks = weights_of(pair_prefix, pair_suffix, merge_count, held_blocks, first_count)
    selected = jnp.einsum(
        "iap,prc->airc", picks, prefix, preferred_element_type=jnp.float32
    ).astype(jnp.bfloat16)
    selected = selected.reshape(first_count, pieces * rows_piece, twice_width)
    half = twice_width // 2
    real = selected[:, :, :half]
    imag = selected[:, :, half:]
    by_real = jnp.einsum(
        "arc,acw->rw", jnp.concatenate([real, -imag], axis=2),
        portion.reshape(first_count, twice_width, half), preferred_element_type=jnp.float32,
    )
    by_imag = jnp.einsum(
        "arc,acw->rw", jnp.concatenate([imag, real], axis=2),
        portion.reshape(first_count, twice_width, half), preferred_element_type=jnp.float32,
    )
    state_real = by_real.astype(jnp.bfloat16)
    state_imag = by_imag.astype(jnp.bfloat16)
    flat = closed_all.reshape(half, -1)
    capw = cap.shape[2]
    stacked = jnp.concatenate([state_real, state_imag], axis=0)
    both = jnp.dot(stacked, flat, preferred_element_type=jnp.float32)
    both = both.reshape(2, pieces, rows_piece, owners, 2, capw)
    named = jnp.sum(
        (routes[:, :, None] == lax.broadcasted_iota(jnp.int32, (pieces, listed, owners), 2)).astype(
            jnp.float32
        ),
        axis=1,
    )
    summed = jnp.sum(both * named[None, :, None, :, None, None], axis=3)
    out_real = summed[0, :, :, 0] - summed[1, :, :, 1]
    out_imag = summed[0, :, :, 1] + summed[1, :, :, 0]
    return jnp.concatenate([out_real, out_imag], axis=-1)


BF = jnp.bfloat16
F32 = jnp.float32


def flip(value, pattern):
    bit = 1
    while bit <= pattern:
        if pattern & bit:
            value = value + bit - 2 * bit * ((value // bit) % 2)
        bit *= 2
    return value


def iota(shape, axis):
    return lax.broadcasted_iota(jnp.int32, shape, axis)


def chain_kernel(
    sizes, q_ref, f_ref, s_ref, cap_ref, out_ref,
    qall, fall, mall, sel, tab, pick, name, gall, acc, pair_out, pair_in, ret_out, ret_in,
    q_send, q_recv, f_send, f_recv, m_send, m_recv, p_send, p_recv, r_send, r_recv,
):
    chips, first_count, held, rows_piece, pieces, depth, half, wide = sizes
    rows = pieces * rows_piece
    held_rows = held * rows_piece
    base = first_count * held
    batch = chips // 2
    me = lax.axis_index("bits")
    core = me % 2
    chip = me // 2
    other = 1 - core
    mate = 2 * chip + other

    def near(pattern):
        return flip(chip, pattern)

    def send(src, dst, send_sem, recv_sem, device):
        return pltpu.make_async_remote_copy(
            src_ref=src, dst_ref=dst, send_sem=send_sem, recv_sem=recv_sem,
            device_id={"bits": device}, device_id_type=pl.DeviceIdType.MESH,
        )

    barrier = pltpu.get_barrier_semaphore()
    pl.semaphore_signal(
        barrier, inc=1, device_id={"bits": mate}, device_id_type=pl.DeviceIdType.MESH
    )
    for t in range(1, chips):
        pl.semaphore_signal(
            barrier, inc=1, device_id={"bits": 2 * near(t) + core},
            device_id_type=pl.DeviceIdType.MESH,
        )

    lane = iota((1, wide), 1)
    sign = jnp.where(lane < wide // 2, -1.0, 1.0).astype(F32)

    def turn(x):
        return pltpu.roll(x, wide // 2, x.ndim - 1) * sign

    closed = jnp.dot(s_ref[0], cap_ref[0], preferred_element_type=F32) + jnp.dot(
        s_ref[1], cap_ref[1], preferred_element_type=F32
    )
    mall[chip] = closed.astype(BF)
    fall[core] = f_ref[...]
    qall[me] = q_ref[chip]

    for a in range(first_count):
        gap = iota((wide, held_rows), 1) - rows_piece * (iota((wide, held_rows), 0) - a * held)
        inside = (gap >= 0) & (gap < rows_piece)
        own = iota((wide, held_rows), 0) < (a + 1) * held
        own = own & (iota((wide, held_rows), 0) >= a * held)
        pick[a] = jnp.where(inside & own, 1.0, 0.0).astype(BF)
    for b in range(2):
        for q in range(batch):
            row = base + 2 * near(2 * q + b) + core
            hit = iota((wide, wide), 0) == row
            name[b, :, q * wide:(q + 1) * wide] = jnp.where(hit, 1.0, 0.0).astype(BF)

    pl.semaphore_wait(barrier, chips)

    def q_direct(t):
        target = near(t)
        return send(q_ref.at[target], qall.at[me], q_send.at[t], q_recv.at[me], 2 * target + core)

    def q_mate():
        return send(q_ref.at[chip], qall.at[me], q_send.at[0], q_recv.at[me], mate)

    def q_pass(t):
        slot = 2 * near(t) + core
        return send(qall.at[slot], qall.at[slot], q_send.at[chips + t], q_recv.at[slot], mate)

    def f_copy(slot):
        return send(f_ref, fall.at[slot], f_send, f_recv, mate)

    def m_copy(slot, index, target):
        return send(
            mall.at[slot], mall.at[slot], m_send.at[index], m_recv.at[slot], 2 * target + core
        )

    lines = [2 * q for q in range(1, batch)]
    for t in range(1, chips):
        q_direct(t).start()
    q_mate().start()
    m_copy(chip, 1, near(1)).start()
    for t in lines:
        m_copy(chip, t, near(t)).start()
    f_copy(core).start()

    def m_arrived(slot):
        m_copy(slot, 0, near(1)).wait_recv()

    def q_arrived(slot):
        send(q_ref.at[chip], qall.at[slot], q_send.at[0], q_recv.at[slot], mate).wait_recv()

    same = (iota((rows, held_rows), 0) - iota((rows, held_rows), 1)) & (rows_piece - 1)
    same = jnp.where(same == 0, 1.0, 0.0).astype(F32)

    def prepare(slot):
        block = qall[slot]
        table = block[held_rows:].astype(F32)[:pieces]
        spread = jnp.broadcast_to(table[:, None, :], (pieces, rows_piece, wide))
        spread = spread.reshape(rows, wide).astype(BF)
        tab[slot] = spread
        for a in range(first_count):
            chosen = jnp.dot(spread, pick[a], preferred_element_type=F32) * same
            sel[slot, :, a * wide:(a + 1) * wide] = jnp.dot(
                chosen.astype(BF), block[:held_rows], preferred_element_type=F32
            ).astype(BF)

    def gather_step(slot, b, q):
        product = jnp.dot(
            fall[...].reshape(4 * first_count * depth, half), mall[slot],
            preferred_element_type=F32,
        ).reshape(2, first_count, 2, depth, wide)
        for c in range(2):
            for a in range(first_count):
                by_real, by_imag = product[c, a, 0], product[c, a, 1]
                at = a * 4 * depth + c * depth
                cols = slice(q * wide, (q + 1) * wide)
                gall[b, at:at + depth, cols] = (by_real + turn(by_imag)).astype(BF)
                gall[b, at + 2 * depth:at + 3 * depth, cols] = (turn(by_real) - by_imag).astype(BF)

    for t in range(1, chips):
        q_arrived(2 * near(t) + core)
        q_pass(t).start()
    f_copy(other).wait_recv()
    gather_step(chip, 0, 0)

    def prepare_own(c, carry):
        prepare(2 * c + core)
        return carry

    def prepare_other(c, carry):
        q_arrived(2 * c + other)
        prepare(2 * c + other)
        return carry

    lax.fori_loop(0, chips, prepare_own, 0)
    for t in lines:
        m_arrived(near(t))
        m_copy(near(t), t + 1, near(1)).start()
        gather_step(near(t), 0, t // 2)
    lax.fori_loop(0, chips, prepare_other, 0)

    def part(slot, b):
        values = jnp.dot(sel[slot], gall[b], preferred_element_type=F32)
        named = jnp.dot(tab[slot], name[b], preferred_element_type=F32)
        values = values * named
        total = values[:, :wide]
        for q in range(1, batch):
            total = total + values[:, q * wide:(q + 1) * wide]
        return total

    def first_half(slot, carry):
        acc[slot] = part(slot, 0)
        return carry

    lax.fori_loop(0, 2 * chips, first_half, 0)
    for q in range(batch):
        m_arrived(near(2 * q + 1))
        gather_step(near(2 * q + 1), 1, q)

    def pair_copy(c):
        return send(pair_out.at[c], pair_in.at[c], p_send.at[c], p_recv.at[c], mate)

    def second_other(c, carry):
        slot = 2 * c + other
        pair_out[c] = (acc[slot] + part(slot, 1)).astype(BF)
        pair_copy(c).start()
        return carry

    def second_own(c, carry):
        slot = 2 * c + core
        acc[slot] = acc[slot] + part(slot, 1)
        return carry

    lax.fori_loop(0, chips, second_other, 0)
    lax.fori_loop(0, chips, second_own, 0)

    def ret_copy(t):
        target = near(t)
        return send(
            ret_out.at[target], ret_in.at[chip], r_send.at[t], r_recv.at[chip], 2 * target + core
        )

    def ret_arrived(source):
        send(
            ret_out.at[source], ret_in.at[source], r_send.at[0], r_recv.at[source],
            2 * source + core,
        ).wait_recv()

    for t in range(chips - 1, 0, -1):
        target = near(t)
        pair_copy(target).wait_recv()
        ret_out[target] = (acc[2 * target + core] + pair_in[target].astype(F32)).astype(BF)
        ret_copy(t).start()
    pair_copy(chip).wait_recv()
    total = acc[me] + pair_in[chip].astype(F32)
    for t in range(1, chips):
        ret_arrived(near(t))
        total = total + ret_in[near(t)].astype(F32)
    out_ref[...] = total

    q_mate().wait_send()
    f_copy(core).wait_send()
    m_copy(chip, 1, near(1)).wait_send()
    for t in lines:
        m_copy(chip, t, near(t)).wait_send()
        m_copy(near(t), t + 1, near(1)).wait_send()
    for t in range(1, chips):
        q_direct(t).wait_send()
        q_pass(t).wait_send()
        ret_copy(t).wait_send()
    for c in range(chips):
        pair_copy(c).wait_send()


def on_device_chain(prefix, first_suffix, pair_prefix, pair_suffix, merge_count, suffix, routes, cap):
    pieces = pair_prefix.shape[0]
    held, rows_piece, twice_width = prefix.shape
    half = twice_width // 2
    first_count, _, depth, _ = first_suffix.shape
    owners = lax.axis_size("bits")
    listed = routes.shape[1]
    chips = owners // 2
    wide = 2 * cap.shape[2]
    rows = pieces * rows_piece
    held_rows = held * rows_piece
    picks = weights_of(pair_prefix, pair_suffix, merge_count, held, first_count)
    named = jnp.sum(
        (routes[:, :, None] == lax.broadcasted_iota(jnp.int32, (pieces, listed, owners), 2)).astype(F32),
        axis=1,
    ).astype(BF)
    table = jnp.concatenate([picks.reshape(pieces, first_count * held), named], axis=1)
    table = jnp.pad(table, ((0, 16 - pieces), (0, wide - table.shape[1])))
    columns = prefix.reshape(held_rows, 2, chips, 2 * depth).transpose(2, 0, 1, 3)
    columns = columns.reshape(chips, held_rows, wide)
    packed = jnp.concatenate(
        [columns, jnp.broadcast_to(table[None], (chips, 16, wide))], axis=1
    )
    caps = jnp.stack(
        [jnp.concatenate([cap[0], cap[1]], axis=1), jnp.concatenate([-cap[1], cap[0]], axis=1)]
    )
    sizes = (chips, first_count, held, rows_piece, pieces, depth, half, wide)
    batch = chips // 2
    vmem = pl.BlockSpec(memory_space=pltpu.VMEM)
    dma = pltpu.SemaphoreType.DMA
    sent = pltpu.VMEM((chips, rows, wide), BF)
    out = pl.pallas_call(
        lambda *refs: chain_kernel(sizes, *refs),
        name="chain",
        out_shape=jax.ShapeDtypeStruct((rows, wide), F32),
        in_specs=[vmem] * 4,
        out_specs=vmem,
        scratch_shapes=[
            pltpu.VMEM((owners, held_rows + 16, wide), BF),
            pltpu.VMEM((2, first_count, 2, depth, half), BF),
            pltpu.VMEM((chips, half, wide), BF),
            pltpu.VMEM((owners, rows, first_count * wide), BF),
            pltpu.VMEM((owners, rows, wide), BF),
            pltpu.VMEM((first_count, wide, held_rows), BF),
            pltpu.VMEM((2, wide, batch * wide), BF),
            pltpu.VMEM((2, first_count * wide, batch * wide), BF),
            pltpu.VMEM((owners, rows, wide), F32),
            sent, sent, sent, sent,
            dma((2 * chips,)), dma((owners,)), dma, dma, dma((chips,)), dma((chips,)),
            dma((chips,)), dma((chips,)), dma((chips,)), dma((chips,)),
        ],
        compiler_params=pltpu.CompilerParams(collective_id=0, has_side_effects=True),
    )(packed, first_suffix, suffix[0], caps)
    return out.reshape(pieces, rows_piece, wide)


def on_device(prefix, first_suffix, pair_prefix, pair_suffix, merge_count, suffix, routes, cap):
    pieces = pair_prefix.shape[0]
    listed = routes.shape[1]
    owners = lax.axis_size("bits")
    slots = min(pieces, max(2, (2 * pieces * listed + owners - 1) // owners))
    chips = owners // 2
    held, rows_piece, twice_width = prefix.shape
    wide = 2 * cap.shape[2]
    fits = (
        owners % 4 == 0 and chips & (chips - 1) == 0 and wide == 128 and pieces == 8
        and twice_width == chips * wide and first_suffix.shape[0] * held + owners <= wide
        and suffix.shape[0] == 1 and rows_piece == 16 and first_suffix.shape[2] % 16 == 0
    )
    body = on_device_sparse
    if slots == pieces:
        body = on_device_chain if fits else on_device_dense
    return body(
        prefix, first_suffix, pair_prefix, pair_suffix, merge_count, suffix, routes, cap
    )


def solution(mesh):
    return jax.shard_map(
        on_device,
        mesh=mesh,
        in_specs=(
            P(("grp", "bits"), None, None),
            P("grp", None, "bits", None),
            P(("grp", "bits"), None),
            P(("grp", "bits"), None),
            P(("grp", "bits")),
            P(("grp", "bits"), None, None, None),
            P(("grp", "bits"), None),
            P(),
        ),
        out_specs=P(("grp", "bits"), None, None),
        check_vma=False,
    )
```

```python
import jax
import jax.numpy as jnp
from jax import lax
from jax.experimental import pallas as pl
from jax.experimental.pallas import tpu as pltpu
from jax.sharding import PartitionSpec as P

HIGHEST_PRECISION = lax.Precision.HIGHEST


def complex_form(blocks):
    real_part = blocks[..., 0, :, :]
    imag_part = blocks[..., 1, :, :]
    upper_half = jnp.concatenate([real_part, imag_part], axis=-1)
    lower_half = jnp.concatenate([-imag_part, real_part], axis=-1)
    return jnp.concatenate([upper_half, lower_half], axis=-2)


def on_device_sparse(prefix, first_suffix, pair_prefix, pair_suffix, merge_count, suffix, routes, cap):
    pieces = pair_prefix.shape[0]
    merges = pair_prefix.shape[1]
    held_blocks = prefix.shape[0]
    rows_piece = prefix.shape[1]
    twice_width = prefix.shape[2]
    half_width = twice_width // 2
    first_count = first_suffix.shape[0]
    listed = routes.shape[1]
    owners = lax.axis_size("bits")
    slot_count = min(pieces, max(2, (2 * pieces * listed + owners - 1) // owners))
    live_mask = lax.broadcasted_iota(jnp.int32, (pieces, merges), 1) < merge_count[:, None]
    matches = (
        pair_suffix[:, :, None] == lax.broadcasted_iota(jnp.int32, (pieces, merges, first_count), 2)
    ) & live_mask[:, :, None]
    which_block = pair_prefix[:, :, None] == lax.broadcasted_iota(
        jnp.int32, (pieces, merges, held_blocks), 2
    )
    prefix_picks = jnp.einsum(
        "ika,ikp->iap", matches.astype(jnp.float32), which_block.astype(jnp.float32)
    ).astype(jnp.bfloat16)
    selected = jnp.einsum(
        "iap,prc->airc", prefix_picks, prefix, preferred_element_type=jnp.float32
    ).astype(jnp.bfloat16)
    selected = selected.reshape(first_count, pieces * rows_piece, twice_width)
    portion = lax.all_gather(first_suffix, "bits", axis=2, tiled=True)
    count_rows = portion.shape[2]
    real_cols = lax.slice_in_dim(selected, 0, count_rows, axis=2)
    imag_cols = lax.dynamic_slice_in_dim(selected, half_width, count_rows, 2)
    left_side = jnp.concatenate([real_cols, imag_cols], axis=2)
    upper_half = jnp.concatenate([portion[:, 0], portion[:, 1]], axis=2)
    lower_half = jnp.concatenate([-portion[:, 1], portion[:, 0]], axis=2)
    right_side = jnp.concatenate([upper_half, lower_half], axis=1)
    state_rows = jnp.einsum(
        "arc,acw->rw", left_side, right_side, preferred_element_type=jnp.float32
    )
    state_rows = state_rows.astype(jnp.bfloat16).reshape(pieces, rows_piece, twice_width)
    named_by = jnp.sum(
        (routes[:, :, None] == lax.broadcasted_iota(jnp.int32, (pieces, listed, owners), 2)).astype(
            jnp.int32
        ),
        axis=1,
    )
    slot_rank = jnp.cumsum(named_by, axis=0) - named_by
    slot_hit = (
        slot_rank[:, :, None] == lax.broadcasted_iota(jnp.int32, (pieces, owners, slot_count), 2)
    ) & (named_by[:, :, None] > 0)
    dispatch = jnp.transpose(slot_hit, (1, 2, 0)).astype(jnp.bfloat16)
    outgoing = jnp.einsum(
        "dmi,irc->dmrc", dispatch, state_rows, preferred_element_type=jnp.float32
    ).astype(jnp.bfloat16)
    own_form = complex_form(suffix[0])
    cap_form = complex_form(cap)
    products = jnp.einsum(
        "smrc,cw->smrw",
        lax.all_to_all(outgoing, "bits", split_axis=0, concat_axis=0, tiled=True),
        own_form,
        preferred_element_type=jnp.float32,
    ).astype(jnp.bfloat16)
    capped_terms = jnp.einsum(
        "smrw,wv->smrv", products, cap_form, preferred_element_type=jnp.float32
    )
    returned = lax.all_to_all(
        capped_terms.astype(jnp.bfloat16), "bits", split_axis=0, concat_axis=0, tiled=True
    ).astype(capped_terms.dtype)
    return jnp.einsum(
        "dmi,dmrv->irv", dispatch.astype(jnp.float32), returned, precision=HIGHEST_PRECISION
    )


def weights_of(pair_prefix, pair_suffix, merge_count, held_blocks, first_count):
    pieces, merges = pair_prefix.shape
    live_mask = lax.broadcasted_iota(jnp.int32, (pieces, merges), 1) < merge_count[:, None]
    matches = (
        pair_suffix[:, :, None] == lax.broadcasted_iota(jnp.int32, (pieces, merges, first_count), 2)
    ) & live_mask[:, :, None]
    which_block = pair_prefix[:, :, None] == lax.broadcasted_iota(
        jnp.int32, (pieces, merges, held_blocks), 2
    )
    return jnp.sum(
        (matches[:, :, :, None] & which_block[:, :, None, :]).astype(jnp.float32), axis=1
    ).astype(jnp.bfloat16)


def on_device_dense(prefix, first_suffix, pair_prefix, pair_suffix, merge_count, suffix, routes, cap):
    pieces = pair_prefix.shape[0]
    held_blocks, rows_piece, twice_width = prefix.shape
    first_count = first_suffix.shape[0]
    owners = lax.axis_size("bits")
    listed = routes.shape[1]
    portion = lax.all_gather(first_suffix, "bits", axis=2, tiled=True)
    cap_form = jnp.concatenate([cap[0], cap[1]], axis=1)
    cap_turn = jnp.concatenate([-cap[1], cap[0]], axis=1)
    closed = (
        jnp.dot(suffix[0, 0], cap_form, preferred_element_type=jnp.float32)
        + jnp.dot(suffix[0, 1], cap_turn, preferred_element_type=jnp.float32)
    ).astype(jnp.bfloat16)
    closed_all = lax.all_gather(closed, "bits", axis=1, tiled=False)
    picks = weights_of(pair_prefix, pair_suffix, merge_count, held_blocks, first_count)
    selected = jnp.einsum(
        "iap,prc->airc", picks, prefix, preferred_element_type=jnp.float32
    ).astype(jnp.bfloat16)
    selected = selected.reshape(first_count, pieces * rows_piece, twice_width)
    half = twice_width // 2
    real = selected[:, :, :half]
    imag = selected[:, :, half:]
    by_real = jnp.einsum(
        "arc,acw->rw", jnp.concatenate([real, -imag], axis=2),
        portion.reshape(first_count, twice_width, half), preferred_element_type=jnp.float32,
    )
    by_imag = jnp.einsum(
        "arc,acw->rw", jnp.concatenate([imag, real], axis=2),
        portion.reshape(first_count, twice_width, half), preferred_element_type=jnp.float32,
    )
    state_real = by_real.astype(jnp.bfloat16)
    state_imag = by_imag.astype(jnp.bfloat16)
    flat = closed_all.reshape(half, -1)
    capw = cap.shape[2]
    stacked = jnp.concatenate([state_real, state_imag], axis=0)
    both = jnp.dot(stacked, flat, preferred_element_type=jnp.float32)
    both = both.reshape(2, pieces, rows_piece, owners, 2, capw)
    named = jnp.sum(
        (routes[:, :, None] == lax.broadcasted_iota(jnp.int32, (pieces, listed, owners), 2)).astype(
            jnp.float32
        ),
        axis=1,
    )
    summed = jnp.sum(both * named[None, :, None, :, None, None], axis=3)
    out_real = summed[0, :, :, 0] - summed[1, :, :, 1]
    out_imag = summed[0, :, :, 1] + summed[1, :, :, 0]
    return jnp.concatenate([out_real, out_imag], axis=-1)


BF = jnp.bfloat16
F32 = jnp.float32


def flip(value, pattern):
    bit = 1
    while bit <= pattern:
        if pattern & bit:
            value = value + bit - 2 * bit * ((value // bit) % 2)
        bit *= 2
    return value


def iota(shape, axis):
    return lax.broadcasted_iota(jnp.int32, shape, axis)


def chain_kernel(
    sizes, q_ref, f_ref, s_ref, cap_ref, out_ref,
    qall, fall, mall, sel, tab, pick, name, gall, acc, pair_out, pair_in, ret_out, ret_in,
    q_send, q_recv, f_send, f_recv, m_send, m_recv, p_send, p_recv, r_send, r_recv,
):
    chips, first_count, held, rows_piece, pieces, depth, half, wide = sizes
    rows = pieces * rows_piece
    held_rows = held * rows_piece
    base = first_count * held
    batch = chips // 2
    bundle = min(4, chips)
    me = lax.axis_index("bits")
    core = me % 2
    chip = me // 2
    other = 1 - core
    mate = 2 * chip + other

    def near(pattern):
        return flip(chip, pattern)

    def send(src, dst, send_sem, recv_sem, device):
        return pltpu.make_async_remote_copy(
            src_ref=src, dst_ref=dst, send_sem=send_sem, recv_sem=recv_sem,
            device_id={"bits": device}, device_id_type=pl.DeviceIdType.MESH,
        )

    barrier = pltpu.get_barrier_semaphore()
    pl.semaphore_signal(
        barrier, inc=1, device_id={"bits": mate}, device_id_type=pl.DeviceIdType.MESH
    )
    for t in range(1, chips):
        pl.semaphore_signal(
            barrier, inc=1, device_id={"bits": 2 * near(t) + core},
            device_id_type=pl.DeviceIdType.MESH,
        )

    lane = iota((1, wide), 1)
    sign = jnp.where(lane < wide // 2, -1.0, 1.0).astype(F32)

    def turn(x):
        return pltpu.roll(x, wide // 2, x.ndim - 1) * sign

    closed = jnp.dot(s_ref[0], cap_ref[0], preferred_element_type=F32) + jnp.dot(
        s_ref[1], cap_ref[1], preferred_element_type=F32
    )
    mall[chip] = closed.astype(BF)
    fall[core] = f_ref[...]
    qall[0, chip] = q_ref[chip]

    for a in range(first_count):
        line = iota((wide, wide), 0) - a * held
        gap = iota((wide, wide), 1) - rows_piece * line
        inside = (gap >= 0) & (gap < rows_piece) & (line >= 0) & (line < held)
        pick[:, a * wide:(a + 1) * wide] = jnp.where(inside, 1.0, 0.0).astype(BF)
    for b in range(2):
        for q in range(batch):
            row = base + 2 * near(2 * q + b) + core
            hit = iota((wide, wide), 0) == row
            name[b, :, q * wide:(q + 1) * wide] = jnp.where(hit, 1.0, 0.0).astype(BF)

    pl.semaphore_wait(barrier, chips)

    def q_direct(t):
        target = near(t)
        return send(
            q_ref.at[target], qall.at[0, chip], q_send.at[t], q_recv.at[0, chip],
            2 * target + core,
        )

    def q_mate():
        return send(q_ref.at[chip], qall.at[1, chip], q_send.at[0], q_recv.at[1, chip], mate)

    def q_pass(t):
        slot = near(t)
        return send(
            qall.at[0, slot], qall.at[1, slot], q_send.at[chips + t], q_recv.at[1, slot], mate
        )

    def f_copy(slot):
        return send(f_ref, fall.at[slot], f_send, f_recv, mate)

    def m_copy(slot, index, target):
        return send(
            mall.at[slot], mall.at[slot], m_send.at[index], m_recv.at[slot], 2 * target + core
        )

    lines = [2 * q for q in range(1, batch)]
    for t in range(1, chips):
        q_direct(t).start()
    q_mate().start()
    m_copy(chip, 1, near(1)).start()
    for t in lines:
        m_copy(chip, t, near(t)).start()
    f_copy(core).start()

    def m_arrived(slot):
        m_copy(slot, 0, near(1)).wait_recv()

    def q_arrived(kind, slot):
        send(
            q_ref.at[chip], qall.at[kind, slot], q_send.at[0], q_recv.at[kind, slot], mate
        ).wait_recv()

    full = first_count * wide
    same = (iota((rows, full), 0) - iota((rows, full), 1)) & (rows_piece - 1)
    same = jnp.where(same == 0, 1.0, 0.0).astype(F32)

    def prepare(kind, group):
        first = group * bundle
        blocks = [qall[kind, first + u] for u in range(bundle)]
        for u, block in enumerate(blocks):
            table = block[held_rows:].astype(F32)[:pieces]
            spread = jnp.broadcast_to(table[:, None, :], (pieces, rows_piece, wide))
            tab[kind, first + u] = spread.reshape(rows, wide).astype(BF)
        spreads = tab[kind, pl.ds(first, bundle)].reshape(bundle * rows, wide)
        chosen = jnp.dot(spreads, pick[...], preferred_element_type=F32)
        for u, block in enumerate(blocks):
            kept = (chosen[u * rows:(u + 1) * rows] * same).astype(BF)
            stacked = jnp.concatenate(
                [kept[:, a * wide:a * wide + held_rows] for a in range(first_count)], axis=0
            )
            picked = jnp.dot(stacked, block[:held_rows], preferred_element_type=F32).astype(BF)
            for a in range(first_count):
                sel[kind, first + u, :, a * wide:(a + 1) * wide] = picked[a * rows:(a + 1) * rows]

    def gather_step(slot, b, q):
        product = jnp.dot(
            fall[...].reshape(4 * first_count * depth, half), mall[slot],
            preferred_element_type=F32,
        ).reshape(2, first_count, 2, depth, wide)
        for c in range(2):
            for a in range(first_count):
                by_real, by_imag = product[c, a, 0], product[c, a, 1]
                at = a * 4 * depth + c * depth
                cols = slice(q * wide, (q + 1) * wide)
                gall[b, at:at + depth, cols] = (by_real + turn(by_imag)).astype(BF)
                gall[b, at + 2 * depth:at + 3 * depth, cols] = (turn(by_real) - by_imag).astype(BF)

    for t in range(1, chips):
        q_arrived(0, near(t))
        q_pass(t).start()
    f_copy(other).wait_recv()
    gather_step(chip, 0, 0)

    def prepare_own(group, carry):
        prepare(0, group)
        return carry

    def prepare_other(group, carry):
        for u in range(bundle):
            q_arrived(1, group * bundle + u)
        prepare(1, group)
        return carry

    groups = chips // bundle
    lax.fori_loop(0, groups, prepare_own, 0)
    for t in lines:
        m_arrived(near(t))
        m_copy(near(t), t + 1, near(1)).start()
        gather_step(near(t), 0, t // 2)
    lax.fori_loop(0, groups, prepare_other, 0)

    def part(kind, group, b):
        first = pl.ds(group * bundle, bundle)
        lines_sel = sel[kind, first].reshape(bundle * rows, full)
        lines_tab = tab[kind, first].reshape(bundle * rows, wide)
        values = jnp.dot(lines_sel, gall[b], preferred_element_type=F32)
        named = jnp.dot(lines_tab, name[b], preferred_element_type=F32)
        values = values * named
        total = values[:, :wide]
        for q in range(1, batch):
            total = total + values[:, q * wide:(q + 1) * wide]
        return total.reshape(bundle, rows, wide)

    for kind in (1, 0):
        def first_half(group, carry):
            acc[kind, pl.ds(group * bundle, bundle)] = part(kind, group, 0)
            return carry

        lax.fori_loop(0, groups, first_half, 0)
    for q in range(batch):
        m_arrived(near(2 * q + 1))
        gather_step(near(2 * q + 1), 1, q)

    def pair_copy(c):
        return send(pair_out.at[c], pair_in.at[c], p_send.at[c], p_recv.at[c], mate)

    def second_other(group, carry):
        first = pl.ds(group * bundle, bundle)
        pair_out[first] = (acc[1, first] + part(1, group, 1)).astype(BF)
        for u in range(bundle):
            pair_copy(group * bundle + u).start()
        return carry

    def second_own(group, carry):
        first = pl.ds(group * bundle, bundle)
        acc[0, first] = acc[0, first] + part(0, group, 1)
        return carry

    lax.fori_loop(0, groups, second_other, 0)
    lax.fori_loop(0, groups, second_own, 0)

    def ret_copy(t):
        target = near(t)
        return send(
            ret_out.at[target], ret_in.at[chip], r_send.at[t], r_recv.at[chip], 2 * target + core
        )

    def ret_arrived(source):
        send(
            ret_out.at[source], ret_in.at[source], r_send.at[0], r_recv.at[source],
            2 * source + core,
        ).wait_recv()

    for t in range(chips - 1, 0, -1):
        target = near(t)
        pair_copy(target).wait_recv()
        ret_out[target] = (acc[0, target] + pair_in[target].astype(F32)).astype(BF)
        ret_copy(t).start()
    pair_copy(chip).wait_recv()
    total = acc[0, chip] + pair_in[chip].astype(F32)
    for t in range(1, chips):
        ret_arrived(near(t))
        total = total + ret_in[near(t)].astype(F32)
    out_ref[...] = total

    q_mate().wait_send()
    f_copy(core).wait_send()
    m_copy(chip, 1, near(1)).wait_send()
    for t in lines:
        m_copy(chip, t, near(t)).wait_send()
        m_copy(near(t), t + 1, near(1)).wait_send()
    for t in range(1, chips):
        q_direct(t).wait_send()
        q_pass(t).wait_send()
        ret_copy(t).wait_send()
    for c in range(chips):
        pair_copy(c).wait_send()


def on_device_chain(prefix, first_suffix, pair_prefix, pair_suffix, merge_count, suffix, routes, cap):
    pieces = pair_prefix.shape[0]
    held, rows_piece, twice_width = prefix.shape
    half = twice_width // 2
    first_count, _, depth, _ = first_suffix.shape
    owners = lax.axis_size("bits")
    listed = routes.shape[1]
    chips = owners // 2
    wide = 2 * cap.shape[2]
    rows = pieces * rows_piece
    held_rows = held * rows_piece
    picks = weights_of(pair_prefix, pair_suffix, merge_count, held, first_count)
    named = jnp.sum(
        (routes[:, :, None] == lax.broadcasted_iota(jnp.int32, (pieces, listed, owners), 2)).astype(F32),
        axis=1,
    ).astype(BF)
    table = jnp.concatenate([picks.reshape(pieces, first_count * held), named], axis=1)
    table = jnp.pad(table, ((0, 16 - pieces), (0, wide - table.shape[1])))
    columns = prefix.reshape(held_rows, 2, chips, 2 * depth).transpose(2, 0, 1, 3)
    columns = columns.reshape(chips, held_rows, wide)
    packed = jnp.concatenate(
        [columns, jnp.broadcast_to(table[None], (chips, 16, wide))], axis=1
    )
    caps = jnp.stack(
        [jnp.concatenate([cap[0], cap[1]], axis=1), jnp.concatenate([-cap[1], cap[0]], axis=1)]
    )
    sizes = (chips, first_count, held, rows_piece, pieces, depth, half, wide)
    batch = chips // 2
    vmem = pl.BlockSpec(memory_space=pltpu.VMEM)
    dma = pltpu.SemaphoreType.DMA
    sent = pltpu.VMEM((chips, rows, wide), BF)
    out = pl.pallas_call(
        lambda *refs: chain_kernel(sizes, *refs),
        name="chain",
        out_shape=jax.ShapeDtypeStruct((rows, wide), F32),
        in_specs=[vmem] * 4,
        out_specs=vmem,
        scratch_shapes=[
            pltpu.VMEM((2, chips, held_rows + 16, wide), BF),
            pltpu.VMEM((2, first_count, 2, depth, half), BF),
            pltpu.VMEM((chips, half, wide), BF),
            pltpu.VMEM((2, chips, rows, first_count * wide), BF),
            pltpu.VMEM((2, chips, rows, wide), BF),
            pltpu.VMEM((wide, first_count * wide), BF),
            pltpu.VMEM((2, wide, batch * wide), BF),
            pltpu.VMEM((2, first_count * wide, batch * wide), BF),
            pltpu.VMEM((2, chips, rows, wide), F32),
            sent, sent, sent, sent,
            dma((2 * chips,)), dma((2, chips)), dma, dma, dma((chips,)), dma((chips,)),
            dma((chips,)), dma((chips,)), dma((chips,)), dma((chips,)),
        ],
        compiler_params=pltpu.CompilerParams(collective_id=0, has_side_effects=True),
    )(packed, first_suffix, suffix[0], caps)
    return out.reshape(pieces, rows_piece, wide)


def on_device(prefix, first_suffix, pair_prefix, pair_suffix, merge_count, suffix, routes, cap):
    pieces = pair_prefix.shape[0]
    listed = routes.shape[1]
    owners = lax.axis_size("bits")
    slots = min(pieces, max(2, (2 * pieces * listed + owners - 1) // owners))
    chips = owners // 2
    held, rows_piece, twice_width = prefix.shape
    wide = 2 * cap.shape[2]
    fits = (
        owners % 4 == 0 and chips & (chips - 1) == 0 and wide == 128 and pieces == 8
        and twice_width == chips * wide and first_suffix.shape[0] * held + owners <= wide
        and suffix.shape[0] == 1 and rows_piece == 16 and first_suffix.shape[2] % 16 == 0
    )
    body = on_device_sparse
    if slots == pieces:
        body = on_device_chain if fits else on_device_dense
    return body(
        prefix, first_suffix, pair_prefix, pair_suffix, merge_count, suffix, routes, cap
    )


def solution(mesh):
    return jax.shard_map(
        on_device,
        mesh=mesh,
        in_specs=(
            P(("grp", "bits"), None, None),
            P("grp", None, "bits", None),
            P(("grp", "bits"), None),
            P(("grp", "bits"), None),
            P(("grp", "bits")),
            P(("grp", "bits"), None, None, None),
            P(("grp", "bits"), None),
            P(),
        ),
        out_specs=P(("grp", "bits"), None, None),
        check_vma=False,
    )
```

```python
import jax
import jax.numpy as jnp
from jax import lax
from jax.experimental import pallas as pl
from jax.experimental.pallas import tpu as pltpu
from jax.sharding import PartitionSpec as P

HIGHEST_PRECISION = lax.Precision.HIGHEST


def complex_form(blocks):
    real_part = blocks[..., 0, :, :]
    imag_part = blocks[..., 1, :, :]
    upper_half = jnp.concatenate([real_part, imag_part], axis=-1)
    lower_half = jnp.concatenate([-imag_part, real_part], axis=-1)
    return jnp.concatenate([upper_half, lower_half], axis=-2)


def on_device_sparse(prefix, first_suffix, pair_prefix, pair_suffix, merge_count, suffix, routes, cap):
    pieces = pair_prefix.shape[0]
    merges = pair_prefix.shape[1]
    held_blocks = prefix.shape[0]
    rows_piece = prefix.shape[1]
    twice_width = prefix.shape[2]
    half_width = twice_width // 2
    first_count = first_suffix.shape[0]
    listed = routes.shape[1]
    owners = lax.axis_size("bits")
    slot_count = min(pieces, max(2, (2 * pieces * listed + owners - 1) // owners))
    live_mask = lax.broadcasted_iota(jnp.int32, (pieces, merges), 1) < merge_count[:, None]
    matches = (
        pair_suffix[:, :, None] == lax.broadcasted_iota(jnp.int32, (pieces, merges, first_count), 2)
    ) & live_mask[:, :, None]
    which_block = pair_prefix[:, :, None] == lax.broadcasted_iota(
        jnp.int32, (pieces, merges, held_blocks), 2
    )
    prefix_picks = jnp.einsum(
        "ika,ikp->iap", matches.astype(jnp.float32), which_block.astype(jnp.float32)
    ).astype(jnp.bfloat16)
    selected = jnp.einsum(
        "iap,prc->airc", prefix_picks, prefix, preferred_element_type=jnp.float32
    ).astype(jnp.bfloat16)
    selected = selected.reshape(first_count, pieces * rows_piece, twice_width)
    portion = lax.all_gather(first_suffix, "bits", axis=2, tiled=True)
    count_rows = portion.shape[2]
    real_cols = lax.slice_in_dim(selected, 0, count_rows, axis=2)
    imag_cols = lax.dynamic_slice_in_dim(selected, half_width, count_rows, 2)
    left_side = jnp.concatenate([real_cols, imag_cols], axis=2)
    upper_half = jnp.concatenate([portion[:, 0], portion[:, 1]], axis=2)
    lower_half = jnp.concatenate([-portion[:, 1], portion[:, 0]], axis=2)
    right_side = jnp.concatenate([upper_half, lower_half], axis=1)
    state_rows = jnp.einsum(
        "arc,acw->rw", left_side, right_side, preferred_element_type=jnp.float32
    )
    state_rows = state_rows.astype(jnp.bfloat16).reshape(pieces, rows_piece, twice_width)
    named_by = jnp.sum(
        (routes[:, :, None] == lax.broadcasted_iota(jnp.int32, (pieces, listed, owners), 2)).astype(
            jnp.int32
        ),
        axis=1,
    )
    slot_rank = jnp.cumsum(named_by, axis=0) - named_by
    slot_hit = (
        slot_rank[:, :, None] == lax.broadcasted_iota(jnp.int32, (pieces, owners, slot_count), 2)
    ) & (named_by[:, :, None] > 0)
    dispatch = jnp.transpose(slot_hit, (1, 2, 0)).astype(jnp.bfloat16)
    outgoing = jnp.einsum(
        "dmi,irc->dmrc", dispatch, state_rows, preferred_element_type=jnp.float32
    ).astype(jnp.bfloat16)
    own_form = complex_form(suffix[0])
    cap_form = complex_form(cap)
    products = jnp.einsum(
        "smrc,cw->smrw",
        lax.all_to_all(outgoing, "bits", split_axis=0, concat_axis=0, tiled=True),
        own_form,
        preferred_element_type=jnp.float32,
    ).astype(jnp.bfloat16)
    capped_terms = jnp.einsum(
        "smrw,wv->smrv", products, cap_form, preferred_element_type=jnp.float32
    )
    returned = lax.all_to_all(
        capped_terms.astype(jnp.bfloat16), "bits", split_axis=0, concat_axis=0, tiled=True
    ).astype(capped_terms.dtype)
    return jnp.einsum(
        "dmi,dmrv->irv", dispatch.astype(jnp.float32), returned, precision=HIGHEST_PRECISION
    )


def weights_of(pair_prefix, pair_suffix, merge_count, held_blocks, first_count):
    pieces, merges = pair_prefix.shape
    live_mask = lax.broadcasted_iota(jnp.int32, (pieces, merges), 1) < merge_count[:, None]
    matches = (
        pair_suffix[:, :, None] == lax.broadcasted_iota(jnp.int32, (pieces, merges, first_count), 2)
    ) & live_mask[:, :, None]
    which_block = pair_prefix[:, :, None] == lax.broadcasted_iota(
        jnp.int32, (pieces, merges, held_blocks), 2
    )
    return jnp.sum(
        (matches[:, :, :, None] & which_block[:, :, None, :]).astype(jnp.float32), axis=1
    ).astype(jnp.bfloat16)


def on_device_dense(prefix, first_suffix, pair_prefix, pair_suffix, merge_count, suffix, routes, cap):
    pieces = pair_prefix.shape[0]
    held_blocks, rows_piece, twice_width = prefix.shape
    first_count = first_suffix.shape[0]
    owners = lax.axis_size("bits")
    listed = routes.shape[1]
    portion = lax.all_gather(first_suffix, "bits", axis=2, tiled=True)
    cap_form = jnp.concatenate([cap[0], cap[1]], axis=1)
    cap_turn = jnp.concatenate([-cap[1], cap[0]], axis=1)
    closed = (
        jnp.dot(suffix[0, 0], cap_form, preferred_element_type=jnp.float32)
        + jnp.dot(suffix[0, 1], cap_turn, preferred_element_type=jnp.float32)
    ).astype(jnp.bfloat16)
    closed_all = lax.all_gather(closed, "bits", axis=1, tiled=False)
    picks = weights_of(pair_prefix, pair_suffix, merge_count, held_blocks, first_count)
    selected = jnp.einsum(
        "iap,prc->airc", picks, prefix, preferred_element_type=jnp.float32
    ).astype(jnp.bfloat16)
    selected = selected.reshape(first_count, pieces * rows_piece, twice_width)
    half = twice_width // 2
    real = selected[:, :, :half]
    imag = selected[:, :, half:]
    by_real = jnp.einsum(
        "arc,acw->rw", jnp.concatenate([real, -imag], axis=2),
        portion.reshape(first_count, twice_width, half), preferred_element_type=jnp.float32,
    )
    by_imag = jnp.einsum(
        "arc,acw->rw", jnp.concatenate([imag, real], axis=2),
        portion.reshape(first_count, twice_width, half), preferred_element_type=jnp.float32,
    )
    state_real = by_real.astype(jnp.bfloat16)
    state_imag = by_imag.astype(jnp.bfloat16)
    flat = closed_all.reshape(half, -1)
    capw = cap.shape[2]
    stacked = jnp.concatenate([state_real, state_imag], axis=0)
    both = jnp.dot(stacked, flat, preferred_element_type=jnp.float32)
    both = both.reshape(2, pieces, rows_piece, owners, 2, capw)
    named = jnp.sum(
        (routes[:, :, None] == lax.broadcasted_iota(jnp.int32, (pieces, listed, owners), 2)).astype(
            jnp.float32
        ),
        axis=1,
    )
    summed = jnp.sum(both * named[None, :, None, :, None, None], axis=3)
    out_real = summed[0, :, :, 0] - summed[1, :, :, 1]
    out_imag = summed[0, :, :, 1] + summed[1, :, :, 0]
    return jnp.concatenate([out_real, out_imag], axis=-1)


BF = jnp.bfloat16
F32 = jnp.float32


def flip(value, pattern):
    bit = 1
    while bit <= pattern:
        if pattern & bit:
            value = value + bit - 2 * bit * ((value // bit) % 2)
        bit *= 2
    return value


def iota(shape, axis):
    return lax.broadcasted_iota(jnp.int32, shape, axis)


def chain_kernel(
    sizes, x_ref, code_ref, count_ref, route_ref, f_ref, s_ref, cap_ref, out_ref,
    q_ref, qall, fall, mall, sel, tab, pick, name, gall, acc, pair_out, pair_in, ret_out, ret_in,
    q_send, q_recv, f_send, f_recv, m_send, m_recv, p_send, p_recv, r_send, r_recv,
):
    chips, first_count, held, rows_piece, pieces, depth, half, wide = sizes
    rows = pieces * rows_piece
    held_rows = held * rows_piece
    base = first_count * held
    batch = chips // 2
    bundle = min(4, chips)
    me = lax.axis_index("bits")
    core = me % 2
    chip = me // 2
    other = 1 - core
    mate = 2 * chip + other

    def near(pattern):
        return flip(chip, pattern)

    def send(src, dst, send_sem, recv_sem, device):
        return pltpu.make_async_remote_copy(
            src_ref=src, dst_ref=dst, send_sem=send_sem, recv_sem=recv_sem,
            device_id={"bits": device}, device_id_type=pl.DeviceIdType.MESH,
        )

    barrier = pltpu.get_barrier_semaphore()
    pl.semaphore_signal(
        barrier, inc=1, device_id={"bits": mate}, device_id_type=pl.DeviceIdType.MESH
    )
    for t in range(1, chips):
        pl.semaphore_signal(
            barrier, inc=1, device_id={"bits": 2 * near(t) + core},
            device_id_type=pl.DeviceIdType.MESH,
        )

    lane = iota((1, wide), 1)
    sign = jnp.where(lane < wide // 2, -1.0, 1.0).astype(F32)

    def turn(x):
        return pltpu.roll(x, wide // 2, x.ndim - 1) * sign

    spot = iota((pieces, wide), 1)
    table = jnp.zeros((pieces, wide), F32)
    for k in range(code_ref.shape[1]):
        hit = (spot == code_ref[:, k:k + 1]) & (count_ref[...] > k)
        table = table + jnp.where(hit, 1.0, 0.0)
    for k in range(route_ref.shape[1]):
        table = table + jnp.where(spot == route_ref[:, k:k + 1] + base, 1.0, 0.0)
    table = jnp.concatenate([table, jnp.zeros((16 - pieces, wide), F32)], axis=0)
    x = x_ref[...].astype(F32)
    for c in range(chips):
        at = c * (wide // 2)
        q_ref[c, :held_rows] = jnp.concatenate(
            [x[:, at:at + wide // 2], x[:, half + at:half + at + wide // 2]], axis=1
        ).astype(BF)
        q_ref[c, held_rows:] = table.astype(BF)

    def times_cap(block):
        return lax.dot_general(
            block, cap_ref[...], (((1,), (1,)), ((), ())), preferred_element_type=F32
        )

    mall[chip] = (times_cap(s_ref[0]) + turn(times_cap(s_ref[1]))).astype(BF)
    fall[core] = f_ref[...]
    qall[0, chip] = q_ref[chip]

    for a in range(first_count):
        line = iota((wide, wide), 0) - a * held
        gap = iota((wide, wide), 1) - rows_piece * line
        inside = (gap >= 0) & (gap < rows_piece) & (line >= 0) & (line < held)
        pick[:, a * wide:(a + 1) * wide] = jnp.where(inside, 1.0, 0.0).astype(BF)
    for b in range(2):
        for q in range(batch):
            row = base + 2 * near(2 * q + b) + core
            hit = iota((wide, wide), 0) == row
            name[b, :, q * wide:(q + 1) * wide] = jnp.where(hit, 1.0, 0.0).astype(BF)

    pl.semaphore_wait(barrier, chips)

    def q_direct(t):
        target = near(t)
        return send(
            q_ref.at[target], qall.at[0, chip], q_send.at[t], q_recv.at[0, chip],
            2 * target + core,
        )

    def q_mate():
        return send(q_ref.at[chip], qall.at[1, chip], q_send.at[0], q_recv.at[1, chip], mate)

    def q_pass(t):
        slot = near(t)
        return send(
            qall.at[0, slot], qall.at[1, slot], q_send.at[chips + t], q_recv.at[1, slot], mate
        )

    def f_copy(slot):
        return send(f_ref, fall.at[slot], f_send, f_recv, mate)

    def m_copy(slot, index, target):
        return send(
            mall.at[slot], mall.at[slot], m_send.at[index], m_recv.at[slot], 2 * target + core
        )

    lines = [2 * q for q in range(1, batch)]
    for t in range(1, chips):
        q_direct(t).start()
    q_mate().start()
    m_copy(chip, 1, near(1)).start()
    for t in lines:
        m_copy(chip, t, near(t)).start()
    f_copy(core).start()

    def m_arrived(slot):
        m_copy(slot, 0, near(1)).wait_recv()

    def q_arrived(kind, slot):
        send(
            q_ref.at[chip], qall.at[kind, slot], q_send.at[0], q_recv.at[kind, slot], mate
        ).wait_recv()

    full = first_count * wide
    same = (iota((rows, full), 0) - iota((rows, full), 1)) & (rows_piece - 1)
    same = jnp.where(same == 0, 1.0, 0.0).astype(F32)

    def prepare(kind, group):
        first = group * bundle
        blocks = [qall[kind, first + u] for u in range(bundle)]
        for u, block in enumerate(blocks):
            table = block[held_rows:].astype(F32)[:pieces]
            spread = jnp.broadcast_to(table[:, None, :], (pieces, rows_piece, wide))
            tab[kind, first + u] = spread.reshape(rows, wide).astype(BF)
        spreads = tab[kind, pl.ds(first, bundle)].reshape(bundle * rows, wide)
        chosen = jnp.dot(spreads, pick[...], preferred_element_type=F32)
        for u, block in enumerate(blocks):
            kept = (chosen[u * rows:(u + 1) * rows] * same).astype(BF)
            stacked = jnp.concatenate(
                [kept[:, a * wide:a * wide + held_rows] for a in range(first_count)], axis=0
            )
            picked = jnp.dot(stacked, block[:held_rows], preferred_element_type=F32).astype(BF)
            for a in range(first_count):
                sel[kind, first + u, :, a * wide:(a + 1) * wide] = picked[a * rows:(a + 1) * rows]

    def gather_step(slot, b, q):
        product = jnp.dot(
            fall[...].reshape(4 * first_count * depth, half), mall[slot],
            preferred_element_type=F32,
        ).reshape(2, first_count, 2, depth, wide)
        for c in range(2):
            for a in range(first_count):
                by_real, by_imag = product[c, a, 0], product[c, a, 1]
                at = a * 4 * depth + c * depth
                cols = slice(q * wide, (q + 1) * wide)
                gall[b, at:at + depth, cols] = (by_real + turn(by_imag)).astype(BF)
                gall[b, at + 2 * depth:at + 3 * depth, cols] = (turn(by_real) - by_imag).astype(BF)

    for t in range(1, chips):
        q_arrived(0, near(t))
        q_pass(t).start()
    f_copy(other).wait_recv()
    gather_step(chip, 0, 0)

    def prepare_own(group, carry):
        prepare(0, group)
        return carry

    def prepare_other(group, carry):
        for u in range(bundle):
            q_arrived(1, group * bundle + u)
        prepare(1, group)
        return carry

    groups = chips // bundle
    lax.fori_loop(0, groups, prepare_own, 0)
    for t in lines:
        m_arrived(near(t))
        m_copy(near(t), t + 1, near(1)).start()
        gather_step(near(t), 0, t // 2)
    lax.fori_loop(0, groups, prepare_other, 0)

    def part(kind, group, b):
        first = pl.ds(group * bundle, bundle)
        lines_sel = sel[kind, first].reshape(bundle * rows, full)
        lines_tab = tab[kind, first].reshape(bundle * rows, wide)
        values = jnp.dot(lines_sel, gall[b], preferred_element_type=F32)
        named = jnp.dot(lines_tab, name[b], preferred_element_type=F32)
        values = values * named
        total = values[:, :wide]
        for q in range(1, batch):
            total = total + values[:, q * wide:(q + 1) * wide]
        return total.reshape(bundle, rows, wide)

    for kind in (1, 0):
        def first_half(group, carry):
            acc[kind, pl.ds(group * bundle, bundle)] = part(kind, group, 0)
            return carry

        lax.fori_loop(0, groups, first_half, 0)
    for q in range(batch):
        m_arrived(near(2 * q + 1))
        gather_step(near(2 * q + 1), 1, q)

    def pair_copy(c):
        return send(pair_out.at[c], pair_in.at[c], p_send.at[c], p_recv.at[c], mate)

    def second_other(group, carry):
        first = pl.ds(group * bundle, bundle)
        pair_out[first] = (acc[1, first] + part(1, group, 1)).astype(BF)
        for u in range(bundle):
            pair_copy(group * bundle + u).start()
        return carry

    def second_own(group, carry):
        first = pl.ds(group * bundle, bundle)
        acc[0, first] = acc[0, first] + part(0, group, 1)
        return carry

    lax.fori_loop(0, groups, second_other, 0)
    lax.fori_loop(0, groups, second_own, 0)

    def ret_copy(t):
        target = near(t)
        return send(
            ret_out.at[target], ret_in.at[chip], r_send.at[t], r_recv.at[chip], 2 * target + core
        )

    def ret_arrived(source):
        send(
            ret_out.at[source], ret_in.at[source], r_send.at[0], r_recv.at[source],
            2 * source + core,
        ).wait_recv()

    for t in range(chips - 1, 0, -1):
        target = near(t)
        pair_copy(target).wait_recv()
        ret_out[target] = (acc[0, target] + pair_in[target].astype(F32)).astype(BF)
        ret_copy(t).start()
    pair_copy(chip).wait_recv()
    total = acc[0, chip] + pair_in[chip].astype(F32)
    for t in range(1, chips):
        ret_arrived(near(t))
        total = total + ret_in[near(t)].astype(F32)
    out_ref[...] = total

    q_mate().wait_send()
    f_copy(core).wait_send()
    m_copy(chip, 1, near(1)).wait_send()
    for t in lines:
        m_copy(chip, t, near(t)).wait_send()
        m_copy(near(t), t + 1, near(1)).wait_send()
    for t in range(1, chips):
        q_direct(t).wait_send()
        q_pass(t).wait_send()
        ret_copy(t).wait_send()
    for c in range(chips):
        pair_copy(c).wait_send()


def on_device_chain(prefix, first_suffix, pair_prefix, pair_suffix, merge_count, suffix, routes, cap):
    pieces = pair_prefix.shape[0]
    held, rows_piece, twice_width = prefix.shape
    half = twice_width // 2
    first_count, _, depth, _ = first_suffix.shape
    owners = lax.axis_size("bits")
    chips = owners // 2
    wide = 2 * cap.shape[2]
    rows = pieces * rows_piece
    held_rows = held * rows_piece
    code = pair_suffix * held + pair_prefix
    count = merge_count[:, None]
    caps = cap.transpose(0, 2, 1).reshape(wide, half)
    sizes = (chips, first_count, held, rows_piece, pieces, depth, half, wide)
    batch = chips // 2
    vmem = pl.BlockSpec(memory_space=pltpu.VMEM)
    dma = pltpu.SemaphoreType.DMA
    sent = pltpu.VMEM((chips, rows, wide), BF)
    out = pl.pallas_call(
        lambda *refs: chain_kernel(sizes, *refs),
        name="chain",
        out_shape=jax.ShapeDtypeStruct((rows, wide), F32),
        in_specs=[vmem] * 7,
        out_specs=vmem,
        scratch_shapes=[
            pltpu.VMEM((chips, held_rows + 16, wide), BF),
            pltpu.VMEM((2, chips, held_rows + 16, wide), BF),
            pltpu.VMEM((2, first_count, 2, depth, half), BF),
            pltpu.VMEM((chips, half, wide), BF),
            pltpu.VMEM((2, chips, rows, first_count * wide), BF),
            pltpu.VMEM((2, chips, rows, wide), BF),
            pltpu.VMEM((wide, first_count * wide), BF),
            pltpu.VMEM((2, wide, batch * wide), BF),
            pltpu.VMEM((2, first_count * wide, batch * wide), BF),
            pltpu.VMEM((2, chips, rows, wide), F32),
            sent, sent, sent, sent,
            dma((2 * chips,)), dma((2, chips)), dma, dma, dma((chips,)), dma((chips,)),
            dma((chips,)), dma((chips,)), dma((chips,)), dma((chips,)),
        ],
        compiler_params=pltpu.CompilerParams(collective_id=0, has_side_effects=True),
    )(prefix.reshape(held_rows, twice_width), code, count, routes, first_suffix, suffix[0], caps)
    return out.reshape(pieces, rows_piece, wide)


def on_device(prefix, first_suffix, pair_prefix, pair_suffix, merge_count, suffix, routes, cap):
    pieces = pair_prefix.shape[0]
    listed = routes.shape[1]
    owners = lax.axis_size("bits")
    slots = min(pieces, max(2, (2 * pieces * listed + owners - 1) // owners))
    chips = owners // 2
    held, rows_piece, twice_width = prefix.shape
    wide = 2 * cap.shape[2]
    fits = (
        owners % 4 == 0 and chips & (chips - 1) == 0 and wide == 128 and pieces == 8
        and twice_width == chips * wide and first_suffix.shape[0] * held + owners <= wide
        and suffix.shape[0] == 1 and rows_piece == 16 and first_suffix.shape[2] % 16 == 0
    )
    body = on_device_sparse
    if slots == pieces:
        body = on_device_chain if fits else on_device_dense
    return body(
        prefix, first_suffix, pair_prefix, pair_suffix, merge_count, suffix, routes, cap
    )


def solution(mesh):
    return jax.shard_map(
        on_device,
        mesh=mesh,
        in_specs=(
            P(("grp", "bits"), None, None),
            P("grp", None, "bits", None),
            P(("grp", "bits"), None),
            P(("grp", "bits"), None),
            P(("grp", "bits")),
            P(("grp", "bits"), None, None, None),
            P(("grp", "bits"), None),
            P(),
        ),
        out_specs=P(("grp", "bits"), None, None),
        check_vma=False,
    )
```
